32 devices in a mesh: parts: 2 (over y), req: 4 (over z), tp: 2 (over x), sp: 2 (over core).
Axes of the slice: x: 2, y: 2, z: 4, core: 2. Of those that a mesh axis runs over, the one named last changes fastest.
Arguments:
- prompt_x: bfloat16 [1024, 16384], P(('parts', 'req', 'sp'), 'tp'), parts along dimension 0, may hold values from -600 to 600
- prompt_b: bfloat16 [1024, 8, 128], P(('parts', 'req', 'sp'), 'tp'), parts along dimension 0, may hold values from -0.5 to 0.5
- prompt_dt: float32 [1024, 256], P(('parts', 'req', 'sp'), 'tp'), parts along dimension 0, may hold values from 0.5 to 2
- cont_x: bfloat16 [8, 256, 16384], P(('parts', 'req'), 'sp', 'tp'), parts along dimension 0, may hold values from -6 to 6
- cont_bc: bfloat16 [8, 256, 2, 8, 128], P(('parts', 'req'), 'sp', None, 'tp'), parts along dimension 0, may hold values from -0.5 to 0.5
- cont_dt: float32 [8, 256, 256], P(('parts', 'req'), 'sp', 'tp'), parts along dimension 0, may hold values from 0.5 to 2
- decay_rate: float32 [256], P('tp'), may hold values from 0.0063476562 to 0.05
- skip_gain: float32 [256], P('tp'), may hold values from 0.5 to 1.5
- norm_gain: float32 [16384], P('tp'), may hold values from 0.25 to 1.75
- steer_vecs: float32 [7, 16384], P(None, 'tp'), may hold values from -3 to 3
- mult_table: float32 [9], replicated, may hold values from -3 to 3
- mult_idx: int32 [8], P(('parts', 'req')), parts along dimension 0, may hold values from 0 to 8
- behav_idx: int32 [8], P(('parts', 'req')), parts along dimension 0, may hold values from 0 to 6
Outputs:
- steered_out: bfloat16 [8, 256, 16384], P(('parts', 'req'), 'sp', 'tp'), parts along dimension 0
The draws below stay inside these ranges and needn't reach their ends.
There are 2 independent parts, one for each index of `parts`. The reference program is written for one: setup_inputs(seed, part) draws one part's arguments, and reference() takes and returns one part's arrays. A program takes and returns all parts, laid end to end along the dimension named above; an argument that names none is the same for every part. Nothing has to cross between parts.
All inputs are finite; a program needn't handle non-finite values.
Results may differ from the reference program's by a relative error of at most 0.008.
Values sent between devices are 32-bit elements; how exact they have to be, the bound alone decides.
A program may use at most 320 MiB of HBM per device.

```python
import math
import jax
import jax.numpy as jnp
from jax import lax

HEADS = 256
HEAD_DIM = 64
GROUPS = 8
STATE = 128
BEHAV = 7
NMULT = 9
PRE_DEV = 64
CONT_DEV = 128
PROMPT = 512
CONT = 256
REQS = 4
N_SP = 2


def draw_prompt_x(key, part):
    distance = (PROMPT - 1 - jnp.arange(PROMPT, dtype=jnp.float32)) / PROMPT
    ramp = jnp.exp(5.0 * distance)[:, None]
    values = jax.random.truncated_normal(key, -4.0, 4.0, (PROMPT, HEADS * HEAD_DIM), jnp.float32)
    return (values * ramp).astype(jnp.bfloat16)


def draw_decay_rate(key, part):
    pick_key, slow_key, fast_key = jax.random.split(key, 3)
    slow = jnp.exp(jax.random.uniform(slow_key, (HEADS,), jnp.float32, jnp.log(3.25), jnp.log(5.55))) / PROMPT
    fast = jnp.exp(jax.random.uniform(fast_key, (HEADS,), jnp.float32, jnp.log(0.02), jnp.log(0.05)))
    quick = jax.random.bernoulli(pick_key, 0.25, (HEADS,))
    return jnp.where(quick, fast, slow)


def place_ends(values, own_key, least, high):
    extent = values.shape
    spot = [jax.random.randint(jax.random.fold_in(own_key, axis), (), 0, extent[axis]) for axis in range(len(extent))]
    values = values.at[tuple(spot)].set(least)
    longest = extent.index(max(extent))
    spot[longest] = (spot[longest] + 1) % extent[longest]
    return values.at[tuple(spot)].set(high)


def shard_levels(own_key, extent, cuts, smallest, high):
    def one(dim, shards_of):
        steps = jax.random.uniform(jax.random.fold_in(jax.random.fold_in(own_key, 6), dim), (shards_of,), jnp.float32, smallest / len(cuts), high / len(cuts))
        return jnp.repeat(jnp.exp(steps), extent[dim] // shards_of).reshape((-1,) + (1,) * (len(extent) - dim - 1))

    level = one(*cuts[0])
    for cut in cuts[1:]:
        level = level * one(*cut)
    return level


def bell_draw(stream_key, extent, deviation, reach, shards=(), kind=jnp.bfloat16):
    result = deviation * jax.random.normal(stream_key, extent, jnp.float32)
    if shards:
        result = result * shard_levels(stream_key, extent, shards, -0.22, 0.18)
    return jnp.clip(result, -reach, reach).astype(kind)


def setup_inputs(seed: int = 0, part: int = 0) -> dict:
    seeds = jax.random.split(jax.random.key(seed), 14)
    own_keys = jax.random.split(jax.random.fold_in(seeds[13], part), 14)
    return {
        "prompt_x": draw_prompt_x(jax.random.fold_in(jax.random.fold_in(seeds[13], part), 71), part),
        "prompt_b": bell_draw(own_keys[1], (PROMPT, GROUPS, STATE), STATE ** -0.5, 0.5, ((0, 8), (1, 2))),
        "prompt_dt": jnp.clip(jnp.exp(math.log(2.0) - 1.3862944 * jax.random.uniform(own_keys[2], (PROMPT, HEADS), jnp.float32) ** shard_levels(own_keys[2], (PROMPT, HEADS), ((0, 8), (1, 2)), -0.2, 0.2)), 0.5, 2.0),
        "cont_x": bell_draw(own_keys[3], (REQS, CONT, HEADS * HEAD_DIM), 1.0, 6.0, ((0, 4), (1, 2), (2, 2))),
        "cont_bc": bell_draw(own_keys[4], (REQS, CONT, 2, GROUPS, STATE), STATE ** -0.5, 0.5, ((0, 4), (1, 2), (3, 2))),
        "cont_dt": jnp.clip(jnp.exp(math.log(2.0) - 1.3862944 * jax.random.uniform(own_keys[5], (REQS, CONT, HEADS), jnp.float32) ** shard_levels(own_keys[5], (REQS, CONT, HEADS), ((0, 4), (1, 2), (2, 2)), -0.2, 0.2)), 0.5, 2.0),
        "decay_rate": draw_decay_rate(jax.random.fold_in(seeds[13], 71), part),
        "skip_gain": jnp.clip(0.5 + 1.0 * jax.random.uniform(seeds[7], (HEADS,), jnp.float32) ** shard_levels(seeds[7], (HEADS,), ((0, 2),), -0.2, 0.2), 0.5, 1.5),
        "norm_gain": jnp.clip(1.0 + 0.15 * jax.random.normal(seeds[8], (HEADS * HEAD_DIM,), jnp.float32), 0.25, 1.75),
        "steer_vecs": bell_draw(seeds[9], (BEHAV, HEADS * HEAD_DIM), 0.5, 3.0, ((1, 2),), jnp.float32),
        "mult_table": jnp.clip(jax.random.uniform(seeds[10], (NMULT,), jnp.float32, -3.0, 3.0), -3.0, 3.0),
        "mult_idx": place_ends(jax.random.randint(own_keys[11], (REQS,), 0, NMULT), jax.random.fold_in(own_keys[11], 1), 0, NMULT - 1).astype(jnp.int32),
        "behav_idx": place_ends(jax.random.randint(own_keys[12], (REQS,), 0, BEHAV), jax.random.fold_in(own_keys[12], 1), 0, BEHAV - 1).astype(jnp.int32),
    }


def block_state(rows_x, rows_b, rows_dt, decay_rate, groups):
    length = rows_x.shape[0]
    head_count = decay_rate.shape[0]
    per_group = head_count // groups
    head_size = rows_x.shape[1] // head_count
    cumulative = jnp.cumsum(-decay_rate[None, :] * rows_dt, axis=0)
    block_total = cumulative[-1]
    weight = jnp.exp(block_total[None, :] - cumulative) * rows_dt
    scaled = (rows_x.astype(jnp.float32).reshape(length, head_count, head_size) * weight[:, :, None]).astype(jnp.bfloat16)
    scaled = scaled.reshape(length, groups, per_group, head_size)
    local_state = jnp.einsum('tgqp,tgn->gqpn', scaled.astype(jnp.float32), rows_b.astype(jnp.float32), precision=lax.Precision.HIGHEST)
    carried = jnp.einsum('tgq,tgn->gqn', weight.reshape(length, groups, per_group), rows_b.astype(jnp.float32), precision=lax.Precision.HIGHEST)
    return (block_total, local_state.reshape(head_count, head_size, -1), carried.reshape(head_count, -1), cumulative)

def intra_block(steered, bmat, cmat, rows_dt, cumulative, groups):
    length = steered.shape[0]
    head_count = rows_dt.shape[1]
    per_group = head_count // groups
    head_size = steered.shape[1] // head_count
    products = jnp.einsum('tgn,sgn->gts', cmat.astype(jnp.float32), bmat.astype(jnp.float32), precision=lax.Precision.HIGHEST)
    lower_mask = lax.broadcasted_iota(jnp.int32, (length, length), 0) >= lax.broadcasted_iota(jnp.int32, (length, length), 1)
    cum_groups = cumulative.reshape(length, groups, per_group).transpose(1, 2, 0)
    step_groups = rows_dt.reshape(length, groups, per_group).transpose(1, 2, 0)
    input_groups = steered.reshape(length, groups, per_group, head_size).transpose(1, 0, 2, 3)

    def one_group(pieces):
        product_one, cum_one, step_one, input_one = pieces
        differ = cum_one[:, :, None] - cum_one[:, None, :]
        decays = jnp.exp(jnp.where(lower_mask[None], differ, -1e+30))
        mixing = (decays * step_one[:, None, :] * product_one[None]).astype(jnp.bfloat16)
        return jnp.einsum('qts,sqp->tqp', mixing.astype(jnp.float32), input_one.astype(jnp.float32), precision=lax.Precision.HIGHEST)
    outputs = lax.map(one_group, (products, cum_groups, step_groups, input_groups))
    return outputs.transpose(1, 0, 2, 3).reshape(length, head_count, head_size)

def reference(prompt_x, prompt_b, prompt_dt, cont_x, cont_bc, cont_dt, decay_rate, skip_gain, norm_gain, steer_vecs, mult_table, mult_idx, behav_idx):
    blocks = PROMPT // PRE_DEV
    width = HEADS * HEAD_DIM
    per_group = HEADS // GROUPS

    def prompt_step(carry_pair, pieces):
        block_x, block_b, block_dt = pieces
        block_total, local_state, carried, cumulative = block_state(block_x, block_b, block_dt, decay_rate, GROUPS)
        decay_all = jnp.exp(block_total)
        return ((decay_all[:, None, None] * carry_pair[0] + local_state, decay_all[:, None] * carry_pair[1] + carried), None)
    zeros_pair = (jnp.zeros((HEADS, HEAD_DIM, STATE), jnp.float32), jnp.zeros((HEADS, STATE), jnp.float32))
    (prefix_state, prefix_carry), unused = lax.scan(prompt_step, zeros_pair, (prompt_x.reshape(blocks, PRE_DEV, width), prompt_b.reshape(blocks, PRE_DEV, GROUPS, STATE), prompt_dt.reshape(blocks, PRE_DEV, HEADS)))

    def one_request(pieces):
        request_x, request_bc, request_dt, mult_one, behav_one = pieces
        multiplier = mult_table[mult_one]
        vector = steer_vecs[behav_one]
        steered = (request_x.astype(jnp.float32) + multiplier * vector[None, :]).astype(jnp.bfloat16)
        incoming = prefix_state + multiplier * vector.reshape(HEADS, HEAD_DIM)[:, :, None] * prefix_carry[:, None, :]
        results = []
        for block_index in range(N_SP):
            first = block_index * CONT_DEV
            rows_x = steered[first:first + CONT_DEV]
            bmat = request_bc[first:first + CONT_DEV, 0]
            cmat = request_bc[first:first + CONT_DEV, 1]
            rows_dt = request_dt[first:first + CONT_DEV]
            block_total, local_state, carried, cumulative = block_state(rows_x, bmat, rows_dt, decay_rate, GROUPS)
            inner = intra_block(rows_x, bmat, cmat, rows_dt, cumulative, GROUPS)
            incoming_round = incoming.astype(jnp.bfloat16).reshape(GROUPS, per_group, HEAD_DIM, STATE)
            from_state = jnp.einsum('tgn,gqpn->tgqp', cmat.astype(jnp.float32), incoming_round.astype(jnp.float32), precision=lax.Precision.HIGHEST).reshape(CONT_DEV, HEADS, HEAD_DIM)
            skipped = skip_gain[None, :, None] * rows_x.astype(jnp.float32).reshape(CONT_DEV, HEADS, HEAD_DIM)
            results.append(inner + jnp.exp(cumulative)[:, :, None] * from_state + skipped)
            incoming = jnp.exp(block_total)[:, None, None] * incoming + local_state
        mixed = jnp.concatenate(results, axis=0).reshape(CONT, width)
        meansq = lax.optimization_barrier(jnp.sum(mixed * mixed, axis=1)) / (HEADS * HEAD_DIM)
        return (mixed * lax.rsqrt(meansq + 1e-05)[:, None] * norm_gain[None, :]).astype(jnp.bfloat16)
    return lax.map(one_request, (cont_x, cont_bc, cont_dt, mult_idx, behav_idx))
```

```python
import jax
import jax.numpy as jnp
from jax import lax
from jax.sharding import PartitionSpec as P

HEADS = 256
HEAD_DIM = 64


def block_state(rows_x, rows_b, rows_dt, decay_rate, groups):
    length = rows_x.shape[0]
    head_count = decay_rate.shape[0]
    per_group = head_count // groups
    head_size = rows_x.shape[1] // head_count
    cumulative = jnp.cumsum(-decay_rate[None, :] * rows_dt, axis=0)
    block_total = cumulative[-1]
    weight = jnp.exp(block_total[None, :] - cumulative) * rows_dt
    scaled = (
        rows_x.astype(jnp.float32).reshape(length, head_count, head_size) * weight[:, :, None]
    ).astype(jnp.bfloat16)
    scaled = scaled.reshape(length, groups, per_group, head_size)
    local_state = jnp.einsum("tgqp,tgn->gqpn", scaled, rows_b, preferred_element_type=jnp.float32)
    carried = jnp.einsum(
        "tgq,tgn->gqn",
        weight.reshape(length, groups, per_group),
        rows_b.astype(jnp.float32),
        precision=lax.Precision.HIGHEST,
    )
    return (
        block_total,
        local_state.reshape(head_count, head_size, -1),
        carried.reshape(head_count, -1),
        cumulative,
    )


def intra_block(steered, bmat, cmat, rows_dt, cumulative, groups):
    length = steered.shape[0]
    head_count = rows_dt.shape[1]
    per_group = head_count // groups
    head_size = steered.shape[1] // head_count
    products = jnp.einsum("tgn,sgn->gts", cmat, bmat, preferred_element_type=jnp.float32)
    lower_mask = lax.broadcasted_iota(jnp.int32, (length, length), 0) >= lax.broadcasted_iota(
        jnp.int32, (length, length), 1
    )
    row_factor = jnp.exp(cumulative).reshape(length, groups, per_group).transpose(1, 2, 0)
    col_factor = (
        (jnp.exp(-cumulative) * rows_dt).reshape(length, groups, per_group).transpose(1, 2, 0)
    )
    full = products[:, None, :, :] * row_factor[:, :, :, None] * col_factor[:, :, None, :]
    mixing = jnp.where(lower_mask[None, None], full, 0.0).astype(jnp.bfloat16)
    input_groups = steered.reshape(length, groups, per_group, head_size)
    outputs = jnp.einsum(
        "gqts,sgqp->tgqp", mixing, input_groups, preferred_element_type=jnp.float32
    )
    return outputs.reshape(length, head_count, head_size)


def local(
    prompt_x,
    prompt_b,
    prompt_dt,
    cont_x,
    cont_bc,
    cont_dt,
    decay_rate,
    skip_gain,
    norm_gain,
    steer_vecs,
    mult_table,
    mult_idx,
    behav_idx,
):
    groups = prompt_b.shape[1]
    head_count = decay_rate.shape[0]
    per_group = head_count // groups
    head_size = norm_gain.shape[0] // head_count
    prompt_total, prompt_state, prompt_carry, unused = block_state(
        prompt_x, prompt_b, prompt_dt, decay_rate, groups
    )
    place = lax.axis_index(("req", "sp"))
    totals = lax.all_gather(prompt_total, ("req", "sp"))
    later = lax.broadcasted_iota(jnp.int32, totals.shape, 0) > place
    remaining = jnp.exp(jnp.sum(jnp.where(later, totals, 0.0), axis=0))
    prefix_state, prefix_carry = lax.psum(
        (remaining[:, None, None] * prompt_state, remaining[:, None] * prompt_carry),
        ("req", "sp"),
    )
    picked = lax.broadcasted_iota(jnp.int32, mult_table.shape, 0) == mult_idx[0]
    multiplier = jnp.sum(jnp.where(picked, mult_table, 0.0))
    choose = lax.broadcasted_iota(jnp.int32, (steer_vecs.shape[0], 1), 0) == behav_idx[0]
    vector = jnp.sum(jnp.where(choose, steer_vecs, 0.0), axis=0)
    steered = (cont_x[0].astype(jnp.float32) + multiplier * vector[None, :]).astype(jnp.bfloat16)
    bmat = cont_bc[0, :, 0]
    cmat = cont_bc[0, :, 1]
    rows_dt = cont_dt[0]
    length = steered.shape[0]
    block_total, local_state, carried, cumulative = block_state(
        steered, bmat, rows_dt, decay_rate, groups
    )
    before_total, before_state = lax.ppermute((block_total, local_state), "sp", [(0, 1)])
    inner = intra_block(steered, bmat, cmat, rows_dt, cumulative, groups)
    start_state = (
        prefix_state
        + multiplier * vector.reshape(head_count, head_size)[:, :, None] * prefix_carry[:, None, :]
    )
    incoming = jnp.exp(before_total)[:, None, None] * start_state + before_state
    incoming_round = incoming.astype(jnp.bfloat16).reshape(groups, per_group, head_size, -1)
    from_state = jnp.einsum(
        "tgn,gqpn->tgqp", cmat, incoming_round, preferred_element_type=jnp.float32
    ).reshape(length, head_count, head_size)
    skipped = skip_gain[None, :, None] * steered.astype(jnp.float32).reshape(
        length, head_count, head_size
    )
    mixed = (inner + jnp.exp(cumulative)[:, :, None] * from_state + skipped).reshape(
        length, head_count * head_size
    )
    squares = jnp.sum(mixed * mixed, axis=1)
    total_squares = lax.psum(squares, "tp")
    meansq = total_squares / (HEADS * HEAD_DIM)
    return (mixed * lax.rsqrt(meansq + 1e-05)[:, None] * norm_gain[None, :]).astype(jnp.bfloat16)[
        None
    ]


def solution(mesh):
    return jax.shard_map(
        local,
        mesh=mesh,
        in_specs=(
            P(("parts", "req", "sp"), "tp"),
            P(("parts", "req", "sp"), "tp", None),
            P(("parts", "req", "sp"), "tp"),
            P(("parts", "req"), "sp", "tp"),
            P(("parts", "req"), "sp", None, "tp", None),
            P(("parts", "req"), "sp", "tp"),
            P("tp"),
            P("tp"),
            P("tp"),
            P(None, "tp"),
            P(),
            P(("parts", "req")),
            P(("parts", "req")),
        ),
        out_specs=P(("parts", "req"), "sp", "tp"),
        check_vma=False,
    )
```

```python
import functools

import jax
import jax.numpy as jnp
from jax import lax
from jax.experimental import pallas as pl
from jax.experimental.pallas import tpu as pltpu
from jax.sharding import PartitionSpec as P

MESH = pl.DeviceIdType.MESH
F32 = jnp.float32
BF16 = jnp.bfloat16
HIGHEST = lax.Precision.HIGHEST
WIDTH = 256


def dot(a, b):
    return jnp.dot(a, b, preferred_element_type=F32)


def halves(value):
    lead = value.astype(BF16)
    rest = (value - lead.astype(F32)).astype(BF16)
    return jnp.concatenate([lead, rest], axis=1)


def running_sum(rows):
    length = rows.shape[0]
    lower = lax.broadcasted_iota(jnp.int32, (length, length), 0) >= lax.broadcasted_iota(
        jnp.int32, (length, length), 1
    )
    return jnp.dot(
        jnp.where(lower, 1.0, 0.0).astype(F32),
        rows,
        precision=HIGHEST,
        preferred_element_type=F32,
    )


def kernel(
    R,
    TP,
    NCK,
    px,
    pbt,
    pdt,
    cx,
    cbt,
    cc,
    cdt,
    rate,
    skip,
    mv,
    out,
    ss,
    whl,
    colhl,
    rowhl,
    row2hl,
    skiphl,
    cterm,
    gmat,
    row2x,
    tots,
    ctot,
    ctot_in,
    st0s,
    st0r,
    s_sib,
    s_rec,
    s_own,
    s_lin,
    s_lout,
    s_rin,
    s_rout,
    s_tot,
    s_ag,
    c_all,
    c_rec,
    c_own,
    c_lin,
    c_lout,
    c_rin,
    c_rout,
    c_tot,
    c_ag,
    incb,
    ssacc,
    ssl,
    t_send,
    t_recv,
    x_send,
    x_recv,
    l_send,
    l_recv,
    r_send,
    r_recv,
    a_send,
    a_recv,
    z_send,
    z_recv,
    d_send,
    d_recv,
    p_send,
    p_recv,
):
    i = lax.axis_index("req")
    s = lax.axis_index("sp")
    x = lax.axis_index("tp")
    me = i * 2 + s
    hr = R - 1 - i
    far = jnp.maximum(i, hr)
    H = pdt.shape[1]
    C = px.shape[1]
    Gd = pbt.shape[0]
    N = pbt.shape[1]
    T = cx.shape[0]
    half = C // 2
    head = C // H
    gw = C // Gd
    per_group = H // Gd
    nh = N // 2
    sib = {"sp": 1 - s}

    def each(count, skip_index, body):
        def turn(j, carry):
            @pl.when(j != skip_index)
            def _():
                body(j)

            return carry

        lax.fori_loop(0, count, turn, 0)

    def peer(j):
        return {"req": j // 2, "sp": j % 2}

    def remote(src, dst, send, recv, device):
        return pltpu.make_async_remote_copy(
            src_ref=src,
            dst_ref=dst,
            send_sem=send,
            recv_sem=recv,
            device_id=device,
            device_id_type=MESH,
        )

    barrier = pltpu.get_barrier_semaphore()
    each(
        2 * R,
        me,
        lambda j: pl.semaphore_signal(barrier, inc=1, device_id=peer(j), device_id_type=MESH),
    )
    each(
        TP,
        x,
        lambda j: pl.semaphore_signal(barrier, inc=1, device_id={"tp": j}, device_id_type=MESH),
    )
    cum = running_sum(-rate[...] * pdt[...])
    total = cum[pdt.shape[0] - 1 :, :]
    tots[me] = jnp.broadcast_to(total, (8, H))
    pl.semaphore_wait(barrier, 2 * R - 1 + TP - 1)

    def tot_copy(j, slot):
        return remote(tots.at[slot], tots.at[slot], t_send.at[j], t_recv.at[slot], peer(j))

    each(2 * R, me, lambda j: tot_copy(j, me).start())

    ccum = running_sum(-rate[...] * cdt[...])
    ctot[...] = jnp.broadcast_to(ccum[T - 1 :, :], (8, H))

    def d_copy():
        return remote(ctot, ctot_in, d_send.at[0], d_recv.at[0], sib)

    @pl.when(s == 0)
    def _():
        d_copy().start()

    colhl[...] = halves(jnp.exp(-ccum) * cdt[...])
    rowhl[...] = halves(jnp.exp(ccum))
    skiphl[...] = halves(jnp.broadcast_to(skip[...], (8, H)))
    ssacc[...] = jnp.zeros_like(ssacc)

    each(2 * R, me, lambda j: tot_copy(j, j).wait_recv())
    every = tots[...]
    after = lax.broadcasted_iota(jnp.int32, every.shape, 0) > me
    suffix = jnp.sum(jnp.where(after, every, 0.0), axis=0)[0:1, :]
    weight = jnp.exp(suffix + total - cum) * pdt[...]
    whl[...] = halves(weight)

    carry = jnp.zeros((N, H), F32)
    lane_group = lax.broadcasted_iota(jnp.int32, (N, H), 1)
    for g in range(Gd):
        inside = (lane_group >= g * per_group) & (lane_group < (g + 1) * per_group)
        part = jnp.dot(
            pbt[g].astype(F32), weight, precision=HIGHEST, preferred_element_type=F32
        )
        carry = jnp.where(inside, part, carry)
    c_all[0] = carry[:nh]
    c_all[1] = carry[nh:]

    def x_copy(src, dst, k):
        return remote(src, dst, x_send.at[k], x_recv.at[k], sib)

    def carry_x():
        return x_copy(c_all.at[1 - s], c_rec, NCK)

    def state_x(k):
        return x_copy(s_sib.at[k], s_rec.at[k], k)

    def l_copy(src, dst, k):
        return remote(src, dst, l_send.at[k], l_recv.at[k], {"req": jnp.minimum(i + 1, R - 1)})

    def r_copy(src, dst, k):
        return remote(src, dst, r_send.at[k], r_recv.at[k], {"req": jnp.maximum(i - 1, 0)})

    def carry_l():
        return l_copy(c_lout, c_lin, NCK)

    def state_l(k):
        return l_copy(s_lout.at[k], s_lin.at[k], k)

    def carry_r():
        return r_copy(c_rout, c_rin, NCK)

    def state_r(k):
        return r_copy(s_rout.at[k], s_rin.at[k], k)

    def carry_a():
        return remote(c_tot, c_ag, a_send.at[NCK], a_recv.at[NCK], sib)

    def state_a(k):
        return remote(s_tot.at[k], s_ag.at[k], a_send.at[k], a_recv.at[k], sib)

    def z_copy(j):
        return remote(st0s.at[j], st0r.at[j], z_send.at[j], z_recv.at[j], sib)

    carry_x().start()

    def chosen(first_head):
        row = lax.broadcasted_iota(jnp.int32, (2 * H, WIDTH), 0)
        row = jnp.where(row >= H, row - H, row)
        shift = head.bit_length() - 1
        col = lax.shift_right_logical(
            lax.broadcasted_iota(jnp.int32, (2 * H, WIDTH), 1), shift
        )
        return jnp.where(row == col + first_head, 1.0, 0.0).astype(BF16)

    def place(owner, k):
        return pl.multiple_of(owner * half + k * WIDTH, WIDTH)

    def slice_at(base):
        return pl.ds(base, WIDTH)

    def prompt_chunk(owner, k):
        base = place(owner, k)
        spread = dot(whl[...], chosen(base // head))
        scaled = (px[:, slice_at(base)].astype(F32) * spread).astype(BF16)
        return dot(pbt[base // gw], scaled)

    def cont_chunk(owner, k):
        base = place(owner, k)
        j = owner * NCK + k
        g = base // gw
        pick = chosen(base // head)
        steered = (cx[:, slice_at(base)].astype(F32) + mv[:, slice_at(base)]).astype(BF16)
        wide = steered.astype(F32)
        scaled = (wide * dot(colhl[...], pick)).astype(BF16)
        inner = dot(gmat[g], scaled)
        gain = dot(skiphl[...], pick)[0:1, :]
        out[:, slice_at(base)] = dot(rowhl[...], pick) * inner + gain * wide
        row2x[j] = dot(row2hl[...], pick)

        @pl.when(s == 0)
        def _():
            st0s[j] = dot(cbt[g], scaled)
            z_copy(j).start()

    def finish(owner, k, ready):
        base = place(owner, k)
        j = owner * NCK + k
        g = base // gw

        @pl.when(s == 0)
        def _():
            incb[...] = ready[k].astype(BF16)

        @pl.when(s == 1)
        def _():
            z_copy(j).wait_recv()
            incb[...] = (ready[k] + st0r[j]).astype(BF16)

        steer = dot(cterm[...], chosen(base // head)) * mv[:, slice_at(base)]
        y = dot(cc[g], incb[...]) + steer
        mixed = out[:, slice_at(base)] + row2x[j] * y
        out[:, slice_at(base)] = mixed
        square = mixed * mixed
        folded = square[:, :128]
        for q in range(1, WIDTH // 128):
            folded = folded + square[:, q * 128 : (q + 1) * 128]
        ssacc[...] += folded

    lower = lax.broadcasted_iota(jnp.int32, (T, T), 0) >= lax.broadcasted_iota(
        jnp.int32, (T, T), 1
    )
    for g in range(Gd):
        gmat[g] = jnp.where(lower, dot(cc[g], cbt[g]), 0.0).astype(BF16)

    @pl.when(s == 0)
    def _():
        row2hl[...] = rowhl[...]

    @pl.when(s == 1)
    def _():
        d_copy().wait_recv()
        row2hl[...] = halves(jnp.exp(ccum + ctot_in[0:1, :]))

    def push_left_sum(own, lin, lout, copy):
        @pl.when(i > 0)
        def _():
            copy().wait_recv()

        @pl.when(i == 0)
        def _():
            lout[...] = own[...]
            copy().start()

        @pl.when((i > 0) & (i < R - 1))
        def _():
            lout[...] = own[...] + lin[...]
            copy().start()

    def push_right_sum(own, rin, rout, copy):
        @pl.when(i < R - 1)
        def _():
            copy().wait_recv()

        @pl.when(i == R - 1)
        def _():
            rout[...] = own[...]
            copy().start()

        @pl.when((i > 0) & (i < R - 1))
        def _():
            rout[...] = own[...] + rin[...]
            copy().start()

    def close(own, lin, rin, tot, copy):
        @pl.when(i == 0)
        def _():
            tot[...] = own[...] + rin[...]

        @pl.when(i == R - 1)
        def _():
            tot[...] = own[...] + lin[...]

        @pl.when((i > 0) & (i < R - 1))
        def _():
            tot[...] = own[...] + lin[...] + rin[...]

        copy().start()

    def within(k):
        return (k >= 0) & (k < NCK)

    def step(m, unused):
        @pl.when(m < NCK)
        def _():
            s_sib[m] = prompt_chunk(1 - s, m)
            state_x(m).start()
            s_own[m] = prompt_chunk(s, m)

        @pl.when(m == 0)
        def _():
            carry_x().wait_recv()
            c_own[...] = c_all[s] + c_rec[...]

        @pl.when(within(m - 1))
        def _():
            state_x(m - 1).wait_recv()
            s_own[m - 1] = s_own[m - 1] + s_rec[m - 1]

        @pl.when(m == i)
        def _():
            push_left_sum(c_own, c_lin, c_lout, carry_l)

        @pl.when(m == hr)
        def _():
            push_right_sum(c_own, c_rin, c_rout, carry_r)

        kl = m - 1 - i

        @pl.when(within(kl))
        def _():
            push_left_sum(
                s_own.at[kl], s_lin.at[kl], s_lout.at[kl], functools.partial(state_l, kl)
            )

        kr = m - 1 - hr

        @pl.when(within(kr))
        def _():
            push_right_sum(
                s_own.at[kr], s_rin.at[kr], s_rout.at[kr], functools.partial(state_r, kr)
            )

        @pl.when(m < NCK)
        def _():
            cont_chunk(s, m)
            cont_chunk(1 - s, m)

        @pl.when(m == far)
        def _():
            close(c_own, c_lin, c_rin, c_tot, carry_a)

        @pl.when(m == far + 1)
        def _():
            carry_a().wait_recv()
            low = jnp.where(s == 0, c_tot[...], c_ag[...])
            high = jnp.where(s == 0, c_ag[...], c_tot[...])
            both = jnp.concatenate([low, high], axis=0)
            lane = lax.broadcasted_iota(jnp.int32, (T, H), 1)
            seen = jnp.zeros((T, H), F32)
            for g in range(Gd):
                inside = (lane >= g * per_group) & (lane < (g + 1) * per_group)
                part = jnp.dot(
                    cc[g].astype(F32), both, precision=HIGHEST, preferred_element_type=F32
                )
                seen = jnp.where(inside, part, seen)
            cterm[...] = halves(seen)

        kt = m - 1 - far

        @pl.when(within(kt))
        def _():
            close(
                s_own.at[kt],
                s_lin.at[kt],
                s_rin.at[kt],
                s_tot.at[kt],
                functools.partial(state_a, kt),
            )
            finish(s, kt, s_tot)

        kf = kt - 1

        @pl.when(within(kf))
        def _():
            state_a(kf).wait_recv()
            finish(1 - s, kf, s_ag)

        return unused

    lax.fori_loop(0, NCK + R + 1, step, 0)

    ssl[x] = lax.dot_general(
        jnp.ones((8, 128), F32),
        ssacc[...],
        (((1,), (1,)), ((), ())),
        precision=HIGHEST,
        preferred_element_type=F32,
    )

    def p_copy(j, slot):
        return remote(ssl.at[slot], ssl.at[slot], p_send.at[j], p_recv.at[slot], {"tp": j})

    each(TP, x, lambda j: p_copy(j, x).start())

    def sent(k, unused):
        state_x(k).wait_send()
        state_a(k).wait_send()

        @pl.when(i < R - 1)
        def _():
            state_l(k).wait_send()

        @pl.when(i > 0)
        def _():
            state_r(k).wait_send()

        @pl.when(s == 0)
        def _():
            z_copy(k).wait_send()
            z_copy(k + NCK).wait_send()

        return unused

    lax.fori_loop(0, NCK, sent, 0)
    carry_x().wait_send()
    carry_a().wait_send()

    @pl.when(i < R - 1)
    def _():
        carry_l().wait_send()

    @pl.when(i > 0)
    def _():
        carry_r().wait_send()

    @pl.when(s == 0)
    def _():
        d_copy().wait_send()

    each(2 * R, me, lambda j: tot_copy(j, me).wait_send())
    each(TP, x, lambda j: p_copy(j, j).wait_recv())
    ss[...] = jnp.sum(ssl[...], axis=0)
    each(TP, x, lambda j: p_copy(j, x).wait_send())


def local(
    prompt_x,
    prompt_b,
    prompt_dt,
    cont_x,
    cont_bc,
    cont_dt,
    decay_rate,
    skip_gain,
    norm_gain,
    steer_vecs,
    mult_table,
    mult_idx,
    behav_idx,
):
    R, TP = lax.axis_size("req"), lax.axis_size("tp")
    H = decay_rate.shape[0]
    tokens, C = prompt_x.shape
    Gd, N = prompt_b.shape[1:]
    T = cont_x.shape[1]
    NCK = C // 2 // WIDTH
    picked = lax.broadcasted_iota(jnp.int32, mult_table.shape, 0) == mult_idx[0]
    multiplier = jnp.sum(jnp.where(picked, mult_table, 0.0))
    choose = lax.broadcasted_iota(jnp.int32, (steer_vecs.shape[0], 1), 0) == behav_idx[0]
    vector = jnp.sum(jnp.where(choose, steer_vecs, 0.0), axis=0)
    args = (
        prompt_x,
        jnp.transpose(prompt_b, (1, 2, 0)),
        prompt_dt,
        cont_x[0],
        jnp.transpose(cont_bc[0, :, 0], (1, 2, 0)),
        jnp.transpose(cont_bc[0, :, 1], (1, 0, 2)),
        cont_dt[0],
        decay_rate[None],
        skip_gain[None],
        (multiplier * vector)[None],
    )
    vmem, dma = pltpu.VMEM, pltpu.SemaphoreType.DMA
    part = (NCK, N, WIDTH)
    carried = (N // 2, H)
    scratch = (
        [vmem((tokens, 2 * H), BF16)]
        + [vmem((T, 2 * H), BF16)] * 3
        + [vmem((8, 2 * H), BF16), vmem((T, 2 * H), BF16), vmem((Gd, T, T), BF16)]
        + [vmem((2 * NCK, T, WIDTH), F32)]
        + [vmem((2 * R, 8, H), F32)]
        + [vmem((8, H), F32)] * 2
        + [vmem((2 * NCK, N, WIDTH), F32)] * 2
        + [vmem(part, F32)] * 9
        + [vmem((2,) + carried, F32)]
        + [vmem(carried, F32)] * 8
        + [vmem((N, WIDTH), BF16), vmem((T, 128), F32), vmem((TP, 8, T), F32)]
        + [dma((2 * R,))] * 2
        + [dma((NCK + 1,))] * 8
        + [dma((2 * NCK,))] * 2
        + [dma((1,))] * 2
        + [dma((TP,))] * 2
    )
    mixed, squares = pl.pallas_call(
        functools.partial(kernel, R, TP, NCK),
        out_shape=(
            jax.ShapeDtypeStruct((T, C), F32),
            jax.ShapeDtypeStruct((8, T), F32),
        ),
        in_specs=[pl.BlockSpec(memory_space=pltpu.VMEM)] * len(args),
        out_specs=(pl.BlockSpec(memory_space=pltpu.VMEM),) * 2,
        scratch_shapes=scratch,
        compiler_params=pltpu.CompilerParams(
            collective_id=0, has_side_effects=True, vmem_limit_bytes=60 * 1024 * 1024
        ),
        name="sweep",
    )(*args)
    meansq = squares[0] / (norm_gain.shape[0] * TP)
    return (mixed * lax.rsqrt(meansq + 1e-05)[:, None] * norm_gain[None, :]).astype(BF16)[None]


def solution(mesh):
    return jax.shard_map(
        local,
        mesh=mesh,
        in_specs=(
            P(("parts", "req", "sp"), "tp"),
            P(("parts", "req", "sp"), "tp", None),
            P(("parts", "req", "sp"), "tp"),
            P(("parts", "req"), "sp", "tp"),
            P(("parts", "req"), "sp", None, "tp", None),
            P(("parts", "req"), "sp", "tp"),
            P("tp"),
            P("tp"),
            P("tp"),
            P(None, "tp"),
            P(),
            P(("parts", "req")),
            P(("parts", "req")),
        ),
        out_specs=P(("parts", "req"), "sp", "tp"),
        check_vma=False,
    )
```

```python
import functools

import jax
import jax.numpy as jnp
from jax import lax
from jax.experimental import pallas as pl
from jax.experimental.pallas import tpu as pltpu
from jax.sharding import PartitionSpec as P

MESH = pl.DeviceIdType.MESH
F32 = jnp.float32
BF16 = jnp.bfloat16
HIGHEST = lax.Precision.HIGHEST
WIDTH = 256
AHEAD = 2
SKEW = 2
LAG = 2


def dot(a, b):
    return jnp.dot(a, b, preferred_element_type=F32)


def halves(value):
    lead = value.astype(BF16)
    rest = (value - lead.astype(F32)).astype(BF16)
    return jnp.concatenate([lead, rest], axis=1)


def running_sum(rows):
    length = rows.shape[0]
    lower = lax.broadcasted_iota(jnp.int32, (length, length), 0) >= lax.broadcasted_iota(
        jnp.int32, (length, length), 1
    )
    return jnp.dot(
        jnp.where(lower, 1.0, 0.0).astype(F32),
        rows,
        precision=HIGHEST,
        preferred_element_type=F32,
    )


def kernel(
    R,
    TP,
    NCK,
    px,
    pb,
    pdt,
    cx,
    cbc,
    cdt,
    rate,
    skip,
    vecs,
    table,
    mult_at,
    behav_at,
    out,
    ss,
    whl,
    colhl,
    rowhl,
    row2hl,
    skiphl,
    cterm,
    gmat,
    row2x,
    tots,
    ctot,
    ctot_in,
    st0s,
    st0r,
    s_sib,
    s_rec,
    s_own,
    s_lin,
    s_lout,
    s_rin,
    s_rout,
    s_tot,
    s_ag,
    c_all,
    c_rec,
    c_own,
    c_lin,
    c_lout,
    c_rin,
    c_rout,
    c_tot,
    c_ag,
    incb,
    ssacc,
    ssl,
    mv,
    pbt,
    cbt,
    cc,
    t_send,
    t_recv,
    x_send,
    x_recv,
    l_send,
    l_recv,
    r_send,
    r_recv,
    a_send,
    a_recv,
    z_send,
    z_recv,
    d_send,
    d_recv,
    p_send,
    p_recv,
):
    i = lax.axis_index("req")
    s = lax.axis_index("sp")
    x = lax.axis_index("tp")
    me = i * 2 + s
    hr = R - 1 - i
    far = jnp.maximum(i, hr)
    H = pdt.shape[1]
    C = px.shape[1]
    Gd, N = pb.shape[1:]
    T = cx.shape[0]
    half = C // 2
    head = C // H
    gw = C // Gd
    per_group = H // Gd
    nh = N // 2
    sib = {"sp": 1 - s}

    def each(count, skip_index, body):
        def turn(j, carry):
            @pl.when(j != skip_index)
            def _():
                body(j)

            return carry

        lax.fori_loop(0, count, turn, 0)

    def peer(j):
        return {"req": j // 2, "sp": j % 2}

    def remote(src, dst, send, recv, device):
        return pltpu.make_async_remote_copy(
            src_ref=src,
            dst_ref=dst,
            send_sem=send,
            recv_sem=recv,
            device_id=device,
            device_id_type=MESH,
        )

    barrier = pltpu.get_barrier_semaphore()
    each(
        2 * R,
        me,
        lambda j: pl.semaphore_signal(barrier, inc=1, device_id=peer(j), device_id_type=MESH),
    )
    each(
        TP,
        x,
        lambda j: pl.semaphore_signal(barrier, inc=1, device_id={"tp": j}, device_id_type=MESH),
    )
    cum = running_sum(-rate[...] * pdt[...])
    total = cum[pdt.shape[0] - 1 :, :]
    tots[me] = jnp.broadcast_to(total, (8, H))
    pl.semaphore_wait(barrier, 2 * R - 1 + TP - 1)

    def tot_copy(j, slot):
        return remote(tots.at[slot], tots.at[slot], t_send.at[j], t_recv.at[slot], peer(j))

    each(2 * R, me, lambda j: tot_copy(j, me).start())

    ccum = running_sum(-rate[...] * cdt[...])
    ctot[...] = jnp.broadcast_to(ccum[T - 1 :, :], (8, H))

    def d_copy():
        return remote(ctot, ctot_in, d_send.at[0], d_recv.at[0], sib)

    @pl.when(s == 0)
    def _():
        d_copy().start()

    colhl[...] = halves(jnp.exp(-ccum) * cdt[...])
    rowhl[...] = halves(jnp.exp(ccum))
    skiphl[...] = halves(jnp.broadcast_to(skip[...], (8, H)))
    ssacc[...] = jnp.zeros_like(ssacc)
    entry = lax.broadcasted_iota(jnp.int32, table.shape, 1) == mult_at[0]
    multiplier = jnp.sum(jnp.where(entry, table[...], 0.0), axis=1, keepdims=True)
    wanted = lax.broadcasted_iota(jnp.int32, vecs.shape, 0) == behav_at[0]
    mv[...] = multiplier * jnp.sum(jnp.where(wanted, vecs[...], 0.0), axis=0, keepdims=True)
    for g in range(Gd):
        pbt[g] = pb[:, g, :].astype(F32).T.astype(BF16)
        cbt[g] = cbc[:, 0, g, :].astype(F32).T.astype(BF16)
        cc[g] = cbc[:, 1, g, :]

    lower = lax.broadcasted_iota(jnp.int32, (T, T), 0) >= lax.broadcasted_iota(
        jnp.int32, (T, T), 1
    )
    for g in range(Gd):
        gmat[g] = jnp.where(lower, dot(cc[g], cbt[g]), 0.0).astype(BF16)

    each(2 * R, me, lambda j: tot_copy(j, j).wait_recv())
    every = tots[...]
    after = lax.broadcasted_iota(jnp.int32, every.shape, 0) > me
    suffix = jnp.sum(jnp.where(after, every, 0.0), axis=0)[0:1, :]
    weight = jnp.exp(suffix + total - cum) * pdt[...]
    whl[...] = halves(weight)

    carry = jnp.zeros((N, H), F32)
    lane_group = lax.broadcasted_iota(jnp.int32, (N, H), 1)
    for g in range(Gd):
        inside = (lane_group >= g * per_group) & (lane_group < (g + 1) * per_group)
        part = jnp.dot(
            pbt[g].astype(F32), weight, precision=HIGHEST, preferred_element_type=F32
        )
        carry = jnp.where(inside, part, carry)
    c_all[0] = carry[:nh]
    c_all[1] = carry[nh:]

    def x_copy(src, dst, k):
        return remote(src, dst, x_send.at[k], x_recv.at[k], sib)

    def carry_x():
        return x_copy(c_all.at[1 - s], c_rec, NCK)

    def state_x(k):
        return x_copy(s_sib.at[k], s_rec.at[k], k)

    def l_copy(src, dst, k):
        return remote(src, dst, l_send.at[k], l_recv.at[k], {"req": jnp.minimum(i + 1, R - 1)})

    def r_copy(src, dst, k):
        return remote(src, dst, r_send.at[k], r_recv.at[k], {"req": jnp.maximum(i - 1, 0)})

    def carry_l():
        return l_copy(c_lout, c_lin, 2 * NCK)

    def state_l(k, q):
        rows = pl.ds(q * nh, nh)
        return l_copy(s_lout.at[k, rows], s_lin.at[k, rows], k + q * NCK)

    def carry_r():
        return r_copy(c_rout, c_rin, 2 * NCK)

    def state_r(k, q):
        rows = pl.ds(q * nh, nh)
        return r_copy(s_rout.at[k, rows], s_rin.at[k, rows], k + q * NCK)

    def carry_a():
        return remote(c_tot, c_ag, a_send.at[NCK], a_recv.at[NCK], sib)

    def state_a(k):
        return remote(s_tot.at[k], s_ag.at[k], a_send.at[k], a_recv.at[k], sib)

    def z_copy(j):
        return remote(st0s.at[j], st0r.at[j], z_send.at[j], z_recv.at[j], sib)

    carry_x().start()

    def chosen(first_head):
        row = lax.broadcasted_iota(jnp.int32, (2 * H, WIDTH), 0)
        row = jnp.where(row >= H, row - H, row)
        shift = head.bit_length() - 1
        col = lax.shift_right_logical(
            lax.broadcasted_iota(jnp.int32, (2 * H, WIDTH), 1), shift
        )
        return jnp.where(row == col + first_head, 1.0, 0.0).astype(BF16)

    def place(owner, k):
        return pl.multiple_of(owner * half + k * WIDTH, WIDTH)

    def slice_at(base):
        return pl.ds(base, WIDTH)

    def prompt_chunk(owner, k):
        base = place(owner, k)
        spread = dot(whl[...], chosen(base // head))
        scaled = (px[:, slice_at(base)].astype(F32) * spread).astype(BF16)
        return dot(pbt[base // gw], scaled)

    def cont_chunk(owner, k):
        base = place(owner, k)
        j = owner * NCK + k
        g = base // gw
        pick = chosen(base // head)
        steered = (cx[:, slice_at(base)].astype(F32) + mv[:, slice_at(base)]).astype(BF16)
        wide = steered.astype(F32)
        scaled = (wide * dot(colhl[...], pick)).astype(BF16)
        inner = dot(gmat[g], scaled)
        gain = dot(skiphl[...], pick)[0:1, :]
        out[:, slice_at(base)] = dot(rowhl[...], pick) * inner + gain * wide
        row2x[j] = dot(row2hl[...], pick)

        @pl.when(s == 0)
        def _():
            st0s[j] = dot(cbt[g], scaled)
            z_copy(j).start()

    def finish(owner, k, ready):
        base = place(owner, k)
        j = owner * NCK + k
        g = base // gw

        @pl.when(s == 0)
        def _():
            incb[...] = ready[k].astype(BF16)

        @pl.when(s == 1)
        def _():
            z_copy(j).wait_recv()
            incb[...] = (ready[k] + st0r[j]).astype(BF16)

        steer = dot(cterm[...], chosen(base // head)) * mv[:, slice_at(base)]
        y = dot(cc[g], incb[...]) + steer
        mixed = out[:, slice_at(base)] + row2x[j] * y
        out[:, slice_at(base)] = mixed
        square = mixed * mixed
        folded = square[:, :128]
        for q in range(1, WIDTH // 128):
            folded = folded + square[:, q * 128 : (q + 1) * 128]
        ssacc[...] += folded

    def push_left_sum(own, lin, lout, copy):
        @pl.when(i > 0)
        def _():
            copy().wait_recv()

        @pl.when(i == 0)
        def _():
            lout[...] = own[...]
            copy().start()

        @pl.when((i > 0) & (i < R - 1))
        def _():
            lout[...] = own[...] + lin[...]
            copy().start()

    def push_right_sum(own, rin, rout, copy):
        @pl.when(i < R - 1)
        def _():
            copy().wait_recv()

        @pl.when(i == R - 1)
        def _():
            rout[...] = own[...]
            copy().start()

        @pl.when((i > 0) & (i < R - 1))
        def _():
            rout[...] = own[...] + rin[...]
            copy().start()

    def close(own, lin, rin, tot, copy):
        @pl.when(i == 0)
        def _():
            tot[...] = own[...] + rin[...]

        @pl.when(i == R - 1)
        def _():
            tot[...] = own[...] + lin[...]

        @pl.when((i > 0) & (i < R - 1))
        def _():
            tot[...] = own[...] + lin[...] + rin[...]

        copy().start()

    def within(k):
        return (k >= 0) & (k < NCK)

    def step(m, unused):
        kb = m - AHEAD

        @pl.when(kb == -1)
        def _():
            carry_x().wait_recv()
            c_own[...] = c_all[s] + c_rec[...]

            @pl.when(s == 0)
            def _():
                row2hl[...] = rowhl[...]

            @pl.when(s == 1)
            def _():
                d_copy().wait_recv()
                row2hl[...] = halves(jnp.exp(ccum + ctot_in[0:1, :]))

        @pl.when(within(kb))
        def _():
            state_x(kb).wait_recv()
            s_own[kb] = s_own[kb] + s_rec[kb]

        kl = kb - SKEW * i
        kr = kb - SKEW * hr
        kt = kb - SKEW * far
        kf = kt - LAG

        @pl.when(kl == -1)
        def _():
            push_left_sum(c_own, c_lin, c_lout, carry_l)

        @pl.when(kr == -1)
        def _():
            push_right_sum(c_own, c_rin, c_rout, carry_r)

        for q in range(2):
            rows = pl.ds(q * nh, nh)

            @pl.when(within(kl))
            def _():
                push_left_sum(
                    s_own.at[kl, rows],
                    s_lin.at[kl, rows],
                    s_lout.at[kl, rows],
                    functools.partial(state_l, kl, q),
                )

            @pl.when(within(kr))
            def _():
                push_right_sum(
                    s_own.at[kr, rows],
                    s_rin.at[kr, rows],
                    s_rout.at[kr, rows],
                    functools.partial(state_r, kr, q),
                )

        @pl.when(m < NCK)
        def _():
            s_sib[m] = prompt_chunk(1 - s, m)
            state_x(m).start()
            s_own[m] = prompt_chunk(s, m)

        @pl.when(within(kb))
        def _():
            cont_chunk(s, kb)
            cont_chunk(1 - s, kb)

        @pl.when(kt == -1)
        def _():
            close(c_own, c_lin, c_rin, c_tot, carry_a)

        @pl.when(kf == -1)
        def _():
            carry_a().wait_recv()
            low = jnp.where(s == 0, c_tot[...], c_ag[...])
            high = jnp.where(s == 0, c_ag[...], c_tot[...])
            both = jnp.concatenate([low, high], axis=0)
            lane = lax.broadcasted_iota(jnp.int32, (T, H), 1)
            seen = jnp.zeros((T, H), F32)
            for g in range(Gd):
                inside = (lane >= g * per_group) & (lane < (g + 1) * per_group)
                part = jnp.dot(
                    cc[g].astype(F32), both, precision=HIGHEST, preferred_element_type=F32
                )
                seen = jnp.where(inside, part, seen)
            cterm[...] = halves(seen)

        @pl.when(within(kt))
        def _():
            close(
                s_own.at[kt],
                s_lin.at[kt],
                s_rin.at[kt],
                s_tot.at[kt],
                functools.partial(state_a, kt),
            )

        @pl.when(within(kf))
        def _():
            finish(s, kf, s_tot)
            state_a(kf).wait_recv()
            finish(1 - s, kf, s_ag)

        return unused

    lax.fori_loop(0, NCK + AHEAD + SKEW * (R - 1) + LAG, step, 0)

    ssl[x] = lax.dot_general(
        jnp.ones((8, 128), F32),
        ssacc[...],
        (((1,), (1,)), ((), ())),
        precision=HIGHEST,
        preferred_element_type=F32,
    )

    def p_copy(j, slot):
        return remote(ssl.at[slot], ssl.at[slot], p_send.at[j], p_recv.at[slot], {"tp": j})

    each(TP, x, lambda j: p_copy(j, x).start())

    def sent(k, unused):
        state_x(k).wait_send()
        state_a(k).wait_send()

        @pl.when(i < R - 1)
        def _():
            state_l(k, 0).wait_send()
            state_l(k, 1).wait_send()

        @pl.when(i > 0)
        def _():
            state_r(k, 0).wait_send()
            state_r(k, 1).wait_send()

        @pl.when(s == 0)
        def _():
            z_copy(k).wait_send()
            z_copy(k + NCK).wait_send()

        return unused

    lax.fori_loop(0, NCK, sent, 0)
    carry_x().wait_send()
    carry_a().wait_send()

    @pl.when(i < R - 1)
    def _():
        carry_l().wait_send()

    @pl.when(i > 0)
    def _():
        carry_r().wait_send()

    @pl.when(s == 0)
    def _():
        d_copy().wait_send()

    each(2 * R, me, lambda j: tot_copy(j, me).wait_send())
    each(TP, x, lambda j: p_copy(j, j).wait_recv())
    ss[...] = jnp.sum(ssl[...], axis=0)
    each(TP, x, lambda j: p_copy(j, x).wait_send())


def local(
    prompt_x,
    prompt_b,
    prompt_dt,
    cont_x,
    cont_bc,
    cont_dt,
    decay_rate,
    skip_gain,
    norm_gain,
    steer_vecs,
    mult_table,
    mult_idx,
    behav_idx,
):
    R, TP = lax.axis_size("req"), lax.axis_size("tp")
    H = decay_rate.shape[0]
    tokens, C = prompt_x.shape
    Gd, N = prompt_b.shape[1:]
    T = cont_x.shape[1]
    NCK = C // 2 // WIDTH
    args = (
        prompt_x,
        prompt_b,
        prompt_dt,
        cont_x[0],
        cont_bc[0],
        cont_dt[0],
        decay_rate[None],
        skip_gain[None],
        steer_vecs,
        mult_table[None],
        mult_idx,
        behav_idx,
    )
    vmem, dma = pltpu.VMEM, pltpu.SemaphoreType.DMA
    part = (NCK, N, WIDTH)
    carried = (N // 2, H)
    scratch = (
        [vmem((tokens, 2 * H), BF16)]
        + [vmem((T, 2 * H), BF16)] * 3
        + [vmem((8, 2 * H), BF16), vmem((T, 2 * H), BF16), vmem((Gd, T, T), BF16)]
        + [vmem((2 * NCK, T, WIDTH), F32)]
        + [vmem((2 * R, 8, H), F32)]
        + [vmem((8, H), F32)] * 2
        + [vmem((2 * NCK, N, WIDTH), F32)] * 2
        + [vmem(part, F32)] * 9
        + [vmem((2,) + carried, F32)]
        + [vmem(carried, F32)] * 8
        + [vmem((N, WIDTH), BF16), vmem((T, 128), F32), vmem((TP, 8, T), F32)]
        + [vmem((1, C), F32), vmem((Gd, N, tokens), BF16)]
        + [vmem((Gd, N, T), BF16), vmem((Gd, T, N), BF16)]
        + [dma((2 * R,))] * 2
        + [dma((NCK + 1,))] * 2
        + [dma((2 * NCK + 1,))] * 4
        + [dma((NCK + 1,))] * 2
        + [dma((2 * NCK,))] * 2
        + [dma((1,))] * 2
        + [dma((TP,))] * 2
    )
    mixed, squares = pl.pallas_call(
        functools.partial(kernel, R, TP, NCK),
        out_shape=(
            jax.ShapeDtypeStruct((T, C), F32),
            jax.ShapeDtypeStruct((8, T), F32),
        ),
        in_specs=[pl.BlockSpec(memory_space=pltpu.VMEM)] * (len(args) - 2)
        + [pl.BlockSpec(memory_space=pltpu.SMEM)] * 2,
        out_specs=(pl.BlockSpec(memory_space=pltpu.VMEM),) * 2,
        scratch_shapes=scratch,
        compiler_params=pltpu.CompilerParams(
            collective_id=0, has_side_effects=True, vmem_limit_bytes=60 * 1024 * 1024
        ),
        name="sweep",
    )(*args)
    meansq = squares[0] / (norm_gain.shape[0] * TP)
    return (mixed * lax.rsqrt(meansq + 1e-05)[:, None] * norm_gain[None, :]).astype(BF16)[None]


def solution(mesh):
    return jax.shard_map(
        local,
        mesh=mesh,
        in_specs=(
            P(("parts", "req", "sp"), "tp"),
            P(("parts", "req", "sp"), "tp", None),
            P(("parts", "req", "sp"), "tp"),
            P(("parts", "req"), "sp", "tp"),
            P(("parts", "req"), "sp", None, "tp", None),
            P(("parts", "req"), "sp", "tp"),
            P("tp"),
            P("tp"),
            P("tp"),
            P(None, "tp"),
            P(),
            P(("parts", "req")),
            P(("parts", "req")),
        ),
        out_specs=P(("parts", "req"), "sp", "tp"),
        check_vma=False,
    )
```

```python
import functools

import jax
import jax.numpy as jnp
from jax import lax
from jax.experimental import pallas as pl
from jax.experimental.pallas import tpu as pltpu
from jax.sharding import PartitionSpec as P

MESH = pl.DeviceIdType.MESH
F32 = jnp.float32
BF16 = jnp.bfloat16
HIGHEST = lax.Precision.HIGHEST
WIDTH = 256
AHEAD = 2
SKEW = 2
LAG = 2


def dot(a, b):
    return jnp.dot(a, b, preferred_element_type=F32)


def halves(value):
    lead = value.astype(BF16)
    rest = (value - lead.astype(F32)).astype(BF16)
    return jnp.concatenate([lead, rest], axis=1)


def running_sum(rows):
    length = rows.shape[0]
    lower = lax.broadcasted_iota(jnp.int32, (length, length), 0) >= lax.broadcasted_iota(
        jnp.int32, (length, length), 1
    )
    return jnp.dot(
        jnp.where(lower, 1.0, 0.0).astype(F32),
        rows,
        precision=HIGHEST,
        preferred_element_type=F32,
    )


def kernel(
    R,
    TP,
    NCK,
    px,
    pb,
    pdt,
    cx,
    cbc,
    cdt,
    rate,
    skip,
    vecs,
    table,
    mult_at,
    behav_at,
    gain_row,
    out,
    whl,
    colhl,
    rowhl,
    row2hl,
    skiphl,
    cterm,
    gmat,
    row2x,
    tots,
    ctot,
    ctot_in,
    st0s,
    st0r,
    s_sib,
    s_rec,
    s_own,
    s_lin,
    s_lout,
    s_rin,
    s_rout,
    s_tot,
    s_ag,
    c_all,
    c_rec,
    c_own,
    c_lin,
    c_lout,
    c_rin,
    c_rout,
    c_tot,
    c_ag,
    incb,
    ssacc,
    ssl,
    mv,
    pbt,
    cbt,
    cc,
    mix,
    t_send,
    t_recv,
    x_send,
    x_recv,
    l_send,
    l_recv,
    r_send,
    r_recv,
    a_send,
    a_recv,
    z_send,
    z_recv,
    d_send,
    d_recv,
    p_send,
    p_recv,
):
    i = lax.axis_index("req")
    s = lax.axis_index("sp")
    x = lax.axis_index("tp")
    me = i * 2 + s
    hr = R - 1 - i
    far = jnp.maximum(i, hr)
    H = pdt.shape[1]
    C = px.shape[1]
    Gd, N = pb.shape[1:]
    T = cx.shape[0]
    half = C // 2
    head = C // H
    gw = C // Gd
    per_group = H // Gd
    nh = N // 2
    sib = {"sp": 1 - s}

    def each(count, skip_index, body):
        def turn(j, carry):
            @pl.when(j != skip_index)
            def _():
                body(j)

            return carry

        lax.fori_loop(0, count, turn, 0)

    def peer(j):
        return {"req": j // 2, "sp": j % 2}

    def remote(src, dst, send, recv, device):
        return pltpu.make_async_remote_copy(
            src_ref=src,
            dst_ref=dst,
            send_sem=send,
            recv_sem=recv,
            device_id=device,
            device_id_type=MESH,
        )

    barrier = pltpu.get_barrier_semaphore()
    each(
        2 * R,
        me,
        lambda j: pl.semaphore_signal(barrier, inc=1, device_id=peer(j), device_id_type=MESH),
    )
    each(
        TP,
        x,
        lambda j: pl.semaphore_signal(barrier, inc=1, device_id={"tp": j}, device_id_type=MESH),
    )
    cum = running_sum(-rate[...] * pdt[...])
    total = cum[pdt.shape[0] - 1 :, :]
    tots[me] = jnp.broadcast_to(total, (8, H))
    pl.semaphore_wait(barrier, 2 * R - 1 + TP - 1)

    def tot_copy(j, slot):
        return remote(tots.at[slot], tots.at[slot], t_send.at[j], t_recv.at[slot], peer(j))

    each(2 * R, me, lambda j: tot_copy(j, me).start())

    ccum = running_sum(-rate[...] * cdt[...])
    ctot[...] = jnp.broadcast_to(ccum[T - 1 :, :], (8, H))

    def d_copy():
        return remote(ctot, ctot_in, d_send.at[0], d_recv.at[0], sib)

    @pl.when(s == 0)
    def _():
        d_copy().start()

    colhl[...] = halves(jnp.exp(-ccum) * cdt[...])
    rowhl[...] = halves(jnp.exp(ccum))
    skiphl[...] = halves(jnp.broadcast_to(skip[...], (8, H)))
    ssacc[...] = jnp.zeros_like(ssacc)
    entry = lax.broadcasted_iota(jnp.int32, table.shape, 1) == mult_at[0]
    multiplier = jnp.sum(jnp.where(entry, table[...], 0.0), axis=1, keepdims=True)
    wanted = lax.broadcasted_iota(jnp.int32, vecs.shape, 0) == behav_at[0]
    mv[...] = multiplier * jnp.sum(jnp.where(wanted, vecs[...], 0.0), axis=0, keepdims=True)
    for g in range(Gd):
        pbt[g] = pb[:, g, :].astype(F32).T.astype(BF16)
        cbt[g] = cbc[:, 0, g, :].astype(F32).T.astype(BF16)
        cc[g] = cbc[:, 1, g, :]

    lower = lax.broadcasted_iota(jnp.int32, (T, T), 0) >= lax.broadcasted_iota(
        jnp.int32, (T, T), 1
    )
    for g in range(Gd):
        gmat[g] = jnp.where(lower, dot(cc[g], cbt[g]), 0.0).astype(BF16)

    each(2 * R, me, lambda j: tot_copy(j, j).wait_recv())
    every = tots[...]
    after = lax.broadcasted_iota(jnp.int32, every.shape, 0) > me
    suffix = jnp.sum(jnp.where(after, every, 0.0), axis=0)[0:1, :]
    weight = jnp.exp(suffix + total - cum) * pdt[...]
    whl[...] = halves(weight)

    carry = jnp.zeros((N, H), F32)
    lane_group = lax.broadcasted_iota(jnp.int32, (N, H), 1)
    for g in range(Gd):
        inside = (lane_group >= g * per_group) & (lane_group < (g + 1) * per_group)
        part = jnp.dot(
            pbt[g].astype(F32), weight, precision=HIGHEST, preferred_element_type=F32
        )
        carry = jnp.where(inside, part, carry)
    c_all[0] = carry[:nh]
    c_all[1] = carry[nh:]

    def x_copy(src, dst, k):
        return remote(src, dst, x_send.at[k], x_recv.at[k], sib)

    def carry_x():
        return x_copy(c_all.at[1 - s], c_rec, NCK)

    def state_x(k):
        return x_copy(s_sib.at[k], s_rec.at[k], k)

    def l_copy(src, dst, k):
        return remote(src, dst, l_send.at[k], l_recv.at[k], {"req": jnp.minimum(i + 1, R - 1)})

    def r_copy(src, dst, k):
        return remote(src, dst, r_send.at[k], r_recv.at[k], {"req": jnp.maximum(i - 1, 0)})

    def carry_l():
        return l_copy(c_lout, c_lin, 2 * NCK)

    def state_l(k, q):
        rows = pl.ds(q * nh, nh)
        return l_copy(s_lout.at[k, rows], s_lin.at[k, rows], k + q * NCK)

    def carry_r():
        return r_copy(c_rout, c_rin, 2 * NCK)

    def state_r(k, q):
        rows = pl.ds(q * nh, nh)
        return r_copy(s_rout.at[k, rows], s_rin.at[k, rows], k + q * NCK)

    def carry_a():
        return remote(c_tot, c_ag, a_send.at[NCK], a_recv.at[NCK], sib)

    def state_a(k):
        return remote(s_tot.at[k], s_ag.at[k], a_send.at[k], a_recv.at[k], sib)

    def z_copy(j):
        return remote(st0s.at[j], st0r.at[j], z_send.at[j], z_recv.at[j], sib)

    carry_x().start()

    def chosen(first_head):
        row = lax.broadcasted_iota(jnp.int32, (2 * H, WIDTH), 0)
        row = jnp.where(row >= H, row - H, row)
        shift = head.bit_length() - 1
        col = lax.shift_right_logical(
            lax.broadcasted_iota(jnp.int32, (2 * H, WIDTH), 1), shift
        )
        return jnp.where(row == col + first_head, 1.0, 0.0).astype(BF16)

    def place(owner, k):
        return pl.multiple_of(owner * half + k * WIDTH, WIDTH)

    def slice_at(base):
        return pl.ds(base, WIDTH)

    def prompt_chunk(owner, k):
        base = place(owner, k)
        spread = dot(whl[...], chosen(base // head))
        scaled = (px[:, slice_at(base)].astype(F32) * spread).astype(BF16)
        return dot(pbt[base // gw], scaled)

    def cont_chunk(owner, k):
        base = place(owner, k)
        j = owner * NCK + k
        g = base // gw
        pick = chosen(base // head)
        steered = (cx[:, slice_at(base)].astype(F32) + mv[:, slice_at(base)]).astype(BF16)
        wide = steered.astype(F32)
        scaled = (wide * dot(colhl[...], pick)).astype(BF16)
        inner = dot(gmat[g], scaled)
        gain = dot(skiphl[...], pick)[0:1, :]
        mix[:, slice_at(base)] = dot(rowhl[...], pick) * inner + gain * wide
        row2x[j] = dot(row2hl[...], pick)

        @pl.when(s == 0)
        def _():
            st0s[j] = dot(cbt[g], scaled)
            z_copy(j).start()

    def finish(owner, k, ready):
        base = place(owner, k)
        j = owner * NCK + k
        g = base // gw

        @pl.when(s == 0)
        def _():
            incb[...] = ready[k].astype(BF16)

        @pl.when(s == 1)
        def _():
            z_copy(j).wait_recv()
            incb[...] = (ready[k] + st0r[j]).astype(BF16)

        steer = dot(cterm[...], chosen(base // head)) * mv[:, slice_at(base)]
        y = dot(cc[g], incb[...]) + steer
        mixed = mix[:, slice_at(base)] + row2x[j] * y
        mix[:, slice_at(base)] = mixed
        square = mixed * mixed
        folded = square[:, :128]
        for q in range(1, WIDTH // 128):
            folded = folded + square[:, q * 128 : (q + 1) * 128]
        ssacc[...] += folded

    def push_left_sum(own, lin, lout, copy):
        @pl.when(i > 0)
        def _():
            copy().wait_recv()

        @pl.when(i == 0)
        def _():
            lout[...] = own[...]
            copy().start()

        @pl.when((i > 0) & (i < R - 1))
        def _():
            lout[...] = own[...] + lin[...]
            copy().start()

    def push_right_sum(own, rin, rout, copy):
        @pl.when(i < R - 1)
        def _():
            copy().wait_recv()

        @pl.when(i == R - 1)
        def _():
            rout[...] = own[...]
            copy().start()

        @pl.when((i > 0) & (i < R - 1))
        def _():
            rout[...] = own[...] + rin[...]
            copy().start()

    def close(own, lin, rin, tot, copy):
        @pl.when(i == 0)
        def _():
            tot[...] = own[...] + rin[...]

        @pl.when(i == R - 1)
        def _():
            tot[...] = own[...] + lin[...]

        @pl.when((i > 0) & (i < R - 1))
        def _():
            tot[...] = own[...] + lin[...] + rin[...]

        copy().start()

    def within(k):
        return (k >= 0) & (k < NCK)

    def step(m, unused):
        kb = m - AHEAD

        @pl.when(kb == -1)
        def _():
            carry_x().wait_recv()
            c_own[...] = c_all[s] + c_rec[...]

            @pl.when(s == 0)
            def _():
                row2hl[...] = rowhl[...]

            @pl.when(s == 1)
            def _():
                d_copy().wait_recv()
                row2hl[...] = halves(jnp.exp(ccum + ctot_in[0:1, :]))

        @pl.when(within(kb))
        def _():
            state_x(kb).wait_recv()
            s_own[kb] = s_own[kb] + s_rec[kb]

        kl = kb - SKEW * i
        kr = kb - SKEW * hr
        kt = kb - SKEW * far
        kf = kt - LAG

        @pl.when(kl == -1)
        def _():
            push_left_sum(c_own, c_lin, c_lout, carry_l)

        @pl.when(kr == -1)
        def _():
            push_right_sum(c_own, c_rin, c_rout, carry_r)

        for q in range(2):
            rows = pl.ds(q * nh, nh)

            @pl.when(within(kl))
            def _():
                push_left_sum(
                    s_own.at[kl, rows],
                    s_lin.at[kl, rows],
                    s_lout.at[kl, rows],
                    functools.partial(state_l, kl, q),
                )

            @pl.when(within(kr))
            def _():
                push_right_sum(
                    s_own.at[kr, rows],
                    s_rin.at[kr, rows],
                    s_rout.at[kr, rows],
                    functools.partial(state_r, kr, q),
                )

        @pl.when(m < NCK)
        def _():
            s_sib[m] = prompt_chunk(1 - s, m)
            state_x(m).start()
            s_own[m] = prompt_chunk(s, m)

        @pl.when(within(kb))
        def _():
            cont_chunk(s, kb)
            cont_chunk(1 - s, kb)

        @pl.when(kt == -1)
        def _():
            close(c_own, c_lin, c_rin, c_tot, carry_a)

        @pl.when(kf == -1)
        def _():
            carry_a().wait_recv()
            low = jnp.where(s == 0, c_tot[...], c_ag[...])
            high = jnp.where(s == 0, c_ag[...], c_tot[...])
            both = jnp.concatenate([low, high], axis=0)
            lane = lax.broadcasted_iota(jnp.int32, (T, H), 1)
            seen = jnp.zeros((T, H), F32)
            for g in range(Gd):
                inside = (lane >= g * per_group) & (lane < (g + 1) * per_group)
                part = jnp.dot(
                    cc[g].astype(F32), both, precision=HIGHEST, preferred_element_type=F32
                )
                seen = jnp.where(inside, part, seen)
            cterm[...] = halves(seen)

        @pl.when(within(kt))
        def _():
            close(
                s_own.at[kt],
                s_lin.at[kt],
                s_rin.at[kt],
                s_tot.at[kt],
                functools.partial(state_a, kt),
            )

        @pl.when(within(kf))
        def _():
            finish(s, kf, s_tot)
            state_a(kf).wait_recv()
            finish(1 - s, kf, s_ag)

        return unused

    lax.fori_loop(0, NCK + AHEAD + SKEW * (R - 1) + LAG, step, 0)

    ssl[x] = lax.dot_general(
        jnp.ones((8, 128), F32),
        ssacc[...],
        (((1,), (1,)), ((), ())),
        precision=HIGHEST,
        preferred_element_type=F32,
    )

    def p_copy(j, slot):
        return remote(ssl.at[slot], ssl.at[slot], p_send.at[j], p_recv.at[slot], {"tp": j})

    each(TP, x, lambda j: p_copy(j, x).start())

    def sent(k, unused):
        state_x(k).wait_send()
        state_a(k).wait_send()

        @pl.when(i < R - 1)
        def _():
            state_l(k, 0).wait_send()
            state_l(k, 1).wait_send()

        @pl.when(i > 0)
        def _():
            state_r(k, 0).wait_send()
            state_r(k, 1).wait_send()

        @pl.when(s == 0)
        def _():
            z_copy(k).wait_send()
            z_copy(k + NCK).wait_send()

        return unused

    lax.fori_loop(0, NCK, sent, 0)
    carry_x().wait_send()
    carry_a().wait_send()

    @pl.when(i < R - 1)
    def _():
        carry_l().wait_send()

    @pl.when(i > 0)
    def _():
        carry_r().wait_send()

    @pl.when(s == 0)
    def _():
        d_copy().wait_send()

    each(2 * R, me, lambda j: tot_copy(j, me).wait_send())
    each(TP, x, lambda j: p_copy(j, j).wait_recv())
    meansq = jnp.sum(ssl[...], axis=0) / (C * TP)
    scale = lax.rsqrt(meansq + 1e-05).T[:, 0:1]

    def emit(j, unused):
        at = pl.ds(pl.multiple_of(j * 512, 512), 512)
        out[:, at] = (mix[:, at] * scale * gain_row[:, at]).astype(BF16)
        return unused

    lax.fori_loop(0, C // 512, emit, 0)
    each(TP, x, lambda j: p_copy(j, x).wait_send())


def local(
    prompt_x,
    prompt_b,
    prompt_dt,
    cont_x,
    cont_bc,
    cont_dt,
    decay_rate,
    skip_gain,
    norm_gain,
    steer_vecs,
    mult_table,
    mult_idx,
    behav_idx,
):
    R, TP = lax.axis_size("req"), lax.axis_size("tp")
    H = decay_rate.shape[0]
    tokens, C = prompt_x.shape
    Gd, N = prompt_b.shape[1:]
    T = cont_x.shape[1]
    NCK = C // 2 // WIDTH
    args = (
        prompt_x,
        prompt_b,
        prompt_dt,
        cont_x[0],
        cont_bc[0],
        cont_dt[0],
        decay_rate[None],
        skip_gain[None],
        steer_vecs,
        mult_table[None],
        mult_idx,
        behav_idx,
        norm_gain[None],
    )
    vmem, dma = pltpu.VMEM, pltpu.SemaphoreType.DMA
    part = (NCK, N, WIDTH)
    carried = (N // 2, H)
    scratch = (
        [vmem((tokens, 2 * H), BF16)]
        + [vmem((T, 2 * H), BF16)] * 3
        + [vmem((8, 2 * H), BF16), vmem((T, 2 * H), BF16), vmem((Gd, T, T), BF16)]
        + [vmem((2 * NCK, T, WIDTH), F32)]
        + [vmem((2 * R, 8, H), F32)]
        + [vmem((8, H), F32)] * 2
        + [vmem((2 * NCK, N, WIDTH), F32)] * 2
        + [vmem(part, F32)] * 9
        + [vmem((2,) + carried, F32)]
        + [vmem(carried, F32)] * 8
        + [vmem((N, WIDTH), BF16), vmem((T, 128), F32), vmem((TP, 8, T), F32)]
        + [vmem((1, C), F32), vmem((Gd, N, tokens), BF16)]
        + [vmem((Gd, N, T), BF16), vmem((Gd, T, N), BF16), vmem((T, C), F32)]
        + [dma((2 * R,))] * 2
        + [dma((NCK + 1,))] * 2
        + [dma((2 * NCK + 1,))] * 4
        + [dma((NCK + 1,))] * 2
        + [dma((2 * NCK,))] * 2
        + [dma((1,))] * 2
        + [dma((TP,))] * 2
    )
    normed = pl.pallas_call(
        functools.partial(kernel, R, TP, NCK),
        out_shape=jax.ShapeDtypeStruct((T, C), BF16),
        in_specs=[pl.BlockSpec(memory_space=pltpu.VMEM)] * (len(args) - 3)
        + [pl.BlockSpec(memory_space=pltpu.SMEM)] * 2
        + [pl.BlockSpec(memory_space=pltpu.VMEM)],
        out_specs=pl.BlockSpec(memory_space=pltpu.VMEM),
        scratch_shapes=scratch,
        compiler_params=pltpu.CompilerParams(
            collective_id=0, has_side_effects=True, vmem_limit_bytes=60 * 1024 * 1024
        ),
        name="sweep",
    )(*args)
    return normed[None]


def solution(mesh):
    return jax.shard_map(
        local,
        mesh=mesh,
        in_specs=(
            P(("parts", "req", "sp"), "tp"),
            P(("parts", "req", "sp"), "tp", None),
            P(("parts", "req", "sp"), "tp"),
            P(("parts", "req"), "sp", "tp"),
            P(("parts", "req"), "sp", None, "tp", None),
            P(("parts", "req"), "sp", "tp"),
            P("tp"),
            P("tp"),
            P("tp"),
            P(None, "tp"),
            P(),
            P(("parts", "req")),
            P(("parts", "req")),
        ),
        out_specs=P(("parts", "req"), "sp", "tp"),
        check_vma=False,
    )
```
